32 devices in a mesh: aux: 8 (over z, core), orb: 2 (over y), rep: 2 (over x).
Axes of the slice: x: 2, y: 2, z: 4, core: 2. Of those that a mesh axis runs over, the one named last changes fastest.
Arguments:
- slab: bfloat16 [4096, 4, 1024], P('aux', None, 'orb'), may hold values from -6 to 6
- occ_density: bfloat16 [1024, 512], P('orb'), may hold values from -0.25 to 0.25
- virt_density: bfloat16 [1024, 512], P('orb'), may hold values from -0.25 to 0.25
- block_mask: int32 [32, 8], P('aux', 'orb'), may hold values 0 or 1
- matching: int32 [2, 8], replicated, may hold values from 0 to 7, as said below
Outputs:
- chi_pair: float32 [2, 4096, 512], P('rep', ('aux', 'orb'))
- chi_self: float32 [4096, 512], P(('aux', 'orb'), 'rep')
The draws below stay inside these ranges and needn't reach their ends.
Inputs may be any that keep to these rules, and one draw needn't show every extreme that they name: `matching`: each row pairs the 8 owners: entry p names the partner of p, the partner's entry names p, and no owner is its own partner.
All inputs are finite; a program needn't handle non-finite values. No bound on the sum of `block_mask` on one device may be relied on, other than what follows from the above.
Results may differ from the reference program's by a relative error of at most 0.0041.
Values may be sent and summed in bfloat16 or wider, within the bound.
A program may use at most 64 MiB of HBM per device.

```python
import math
import jax
import jax.numpy as jnp
from jax import lax

BLOCK = 128
AUX_DEV = 512
ORB_DEV = 512
KB = 4
OWNERS = 8
ROUNDS = 2
NAUX = 4096
NORB = 1024
N_ORB = 2


def draw_matching(key, part):
    listed = []
    for round_no in range(ROUNDS):
        shuffled = jax.random.permutation(jax.random.fold_in(key, 11 + round_no), OWNERS).astype(jnp.int32)
        leaders = shuffled[0::2]
        followers = shuffled[1::2]
        partner = jnp.zeros((OWNERS,), jnp.int32).at[leaders].set(followers).at[followers].set(leaders)
        listed.append(partner)
    return jnp.stack(listed).astype(jnp.int32)


def place_ends(entries, stream_key, smallest, top_value):
    longest = entries.shape.index(max(entries.shape))
    spots = []
    for shift in (0, 1):
        where = [jax.random.randint(jax.random.fold_in(stream_key, axis), (), 0, length) for axis, length in enumerate(entries.shape)]
        where[longest] = (where[longest] + shift) % entries.shape[longest]
        spots.append(tuple(where))
    return entries.at[spots[0]].set(smallest).at[spots[1]].set(top_value)


def levels(stream_key, extent, pieces, smallest, top_value):
    level, own = 1.0, jax.random.fold_in(stream_key, 6)
    for dim, blocks in pieces:
        draws = jnp.exp(jax.random.uniform(jax.random.fold_in(own, dim), (blocks,), jnp.float32, smallest / len(pieces), top_value / len(pieces)))
        level = level * jnp.repeat(draws, extent[dim] // blocks).reshape([-1 if axis == dim else 1 for axis in range(len(extent))])
    return level


def centred(own_key, dims, scale, limit, split=(), kind=jnp.bfloat16):
    values = scale * jax.random.normal(own_key, dims, jnp.float32)
    if split:
        values = values * levels(own_key, dims, split, -0.22, 0.18)
    return jnp.clip(values, -limit, limit).astype(kind)


def setup_inputs(seed: int = 0) -> dict:
    seeds = jax.random.split(jax.random.key(seed), 6)
    slab = centred(seeds[0], (NAUX, KB, NORB), 1.0, 6.0, ((0, 8), (2, 2)))
    occ_density = centred(seeds[1], (NORB, ORB_DEV), ORB_DEV ** -0.5, 0.25, ((0, 2),))
    virt_density = centred(seeds[2], (NORB, ORB_DEV), ORB_DEV ** -0.5, 0.25, ((0, 2),))
    block_mask = place_ends((jax.random.randint(seeds[3], (NAUX // BLOCK, NORB // BLOCK), 0, 2) < 1).astype(jnp.int32), jax.random.fold_in(seeds[3], 1), 0, 1)
    matching = draw_matching(jax.random.fold_in(seeds[5], 71), 0)
    return dict(slab=slab, occ_density=occ_density, virt_density=virt_density, block_mask=block_mask, matching=matching)


def transform(density, rows, mask_rows):
    masked = rows * mask_rows[:, None, :]
    blocks = masked.astype(jnp.float32).reshape(AUX_DEV, KB, N_ORB, ORB_DEV)
    dens = density.astype(jnp.float32).reshape(N_ORB, ORB_DEV, ORB_DEV)
    result = jnp.einsum('plbu,but->plbt', blocks, dens)
    return result.reshape(AUX_DEV, KB, NORB).astype(jnp.bfloat16)

def reference(slab, occ_density, virt_density, block_mask, matching):
    factor = 1.0 / math.sqrt(KB * NORB)
    spread = jnp.repeat(jnp.repeat(block_mask.astype(jnp.bfloat16), BLOCK, axis=0), BLOCK, axis=1)
    slab_owned = slab.reshape(OWNERS, AUX_DEV, KB, NORB)
    mask_owned = spread.reshape(OWNERS, AUX_DEV, NORB)
    virtual = lax.map(lambda pair: transform(virt_density, pair[0], pair[1]), (slab_owned, mask_owned))
    virtual = virtual.reshape(OWNERS, AUX_DEV, KB * NORB)

    def one_owner(owner):
        occupied = transform(occ_density, slab_owned[owner], mask_owned[owner]).reshape(AUX_DEV, KB * NORB)
        self_tile = jnp.dot(occupied, virtual[owner].T, preferred_element_type=jnp.float32) * factor

        def round_tile(partner):
            return jnp.dot(occupied, virtual[partner].T, preferred_element_type=jnp.float32) * factor
        pair_tiles = lax.map(round_tile, matching[:, owner])
        return (pair_tiles, self_tile)
    pair_tiles, self_tiles = lax.map(one_owner, jnp.arange(OWNERS, dtype=jnp.int32))
    chi_pair = jnp.transpose(pair_tiles, (1, 0, 2, 3)).reshape(ROUNDS, NAUX, AUX_DEV)
    chi_self = self_tiles.reshape(NAUX, AUX_DEV)
    return (chi_pair, chi_self)
```

```python
import functools
import math

import jax
import jax.numpy as jnp
from jax import lax
from jax.experimental import pallas as pl
from jax.experimental.pallas import tpu as pltpu
from jax.sharding import PartitionSpec as P

BLOCK = 128
MESH = pl.DeviceIdType.MESH
CONTRACT = (((1,), (1,)), ((), ()))
F32, BF16 = jnp.float32, jnp.bfloat16


def kernel(sizes, factor, match_ref, mask_ref, slab, occ_hbm, virt_hbm, pair_out, self_out, *scratch):
    chips, orbs, reps, pieces, groups, chunk = sizes
    gath = scratch[:groups]
    (raw, masked, occ_dens, virt_dens, occ, parts, end_parts, whole, arrived, end_arrived,
     self_parts, self_whole, self_arrived, raw_sem, dens_sem, local_sem, send_sem, recv_sem,
     core_send, core_recv, part_send, part_recv, end_send, end_recv, self_send, self_recv) = scratch[groups:]
    half, aux_rows, orb_cols = masked.shape
    rows_piece = aux_rows // pieces
    per_group = pieces // groups
    cols_group = aux_rows // groups
    rows_out = aux_rows // orbs
    self_cols = aux_rows // reps
    peers = orbs * reps

    a = lax.axis_index("aux")
    o = lax.axis_index("orb")
    r = lax.axis_index("rep")
    z = a // 2
    k = a % 2
    inner = jnp.logical_and(z >= 1, z <= chips - 2)
    at_end = jnp.logical_not(inner)
    feeds = jnp.logical_or(z == 1, z == chips - 2)
    end_aux = jnp.where(z == 1, k, 2 * (chips - 1) + k)
    feed_aux = jnp.where(z == 0, 2 + k, 2 * (chips - 2) + k)
    other = 2 * z + 1 - k

    def peer(j):
        to_orb, to_rep = (o + j // reps) % orbs, (r + j % reps) % reps
        return to_orb, {"orb": to_orb, "rep": to_rep}

    def rows(c):
        return pl.ds(c * rows_piece, rows_piece)

    def raw_copy(c):
        return pltpu.make_async_copy(slab.at[rows(c)], raw.at[rows(c)], raw_sem.at[c])

    for c in range(pieces):
        raw_copy(c).start()
    occ_copy = pltpu.make_async_copy(occ_hbm, occ_dens, dens_sem.at[0])
    virt_copy = pltpu.make_async_copy(virt_hbm, virt_dens, dens_sem.at[1])
    occ_copy.start()
    virt_copy.start()

    barrier = pltpu.get_barrier_semaphore()

    def greet(where):
        pl.semaphore_signal(barrier, inc=1, device_id=where, device_id_type=MESH)

    for d in range(1, chips):
        @pl.when(jnp.logical_and(z - d >= 0, jnp.logical_or(inner, z - d >= 1)))
        def _():
            greet({"aux": a - 2 * d})

        @pl.when(jnp.logical_and(z + d <= chips - 1, jnp.logical_or(inner, z + d <= chips - 2)))
        def _():
            greet({"aux": a + 2 * d})

    greet({"aux": other})
    for j in range(1, peers):
        greet(peer(j)[1])

        @pl.when(feeds)
        def _():
            greet(dict(peer(j)[1], aux=end_aux))

        @pl.when(at_end)
        def _():
            greet(dict(peer(j)[1], aux=feed_aux))

    def remote(src, dst, send, recv, where):
        return pltpu.make_async_remote_copy(
            src_ref=src, dst_ref=dst, send_sem=send, recv_sem=recv, device_id=where, device_id_type=MESH
        )

    def piece(c):
        return masked.at[:, rows(c), :]

    def slot(c, owner):
        return gath[c // per_group].at[owner, :, pl.ds(c % per_group * rows_piece, rows_piece), :]

    def direct(c, source, target):
        return remote(piece(c), slot(c, 2 * source + k), send_sem.at[c, target], recv_sem.at[c, source],
                      {"aux": 2 * target + k})

    def cross(c, zz, src):
        return remote(src, slot(c, 2 * zz + k), core_send.at[c, zz], core_recv.at[c, zz], {"aux": other})

    def local(c):
        return pltpu.make_async_copy(piece(c), slot(c, a), local_sem.at[c])

    def sends(c, d, wait):
        for step in (-d, d):
            target = z + step

            @pl.when(jnp.logical_and(target >= 1, target <= chips - 2))
            def _():
                copy = direct(c, z, jnp.clip(target, 0, chips - 1))
                if wait:
                    copy.wait_send()
                else:
                    copy.start()

    def arrive(c, d):
        for step in (-d, d):
            source = z + step

            @pl.when(jnp.logical_and(inner, jnp.logical_and(source >= 0, source <= chips - 1)))
            def _():
                zz = jnp.clip(source, 0, chips - 1)
                direct(c, zz, z).wait_recv()
                cross(c, zz, slot(c, 2 * zz + k)).start()

    def part_copy(g, j):
        to_orb, where = peer(j)
        return remote(parts.at[g, j % reps, pl.ds(to_orb * rows_out, rows_out), :], arrived.at[g, j - 1],
                      part_send.at[g, j - 1], part_recv.at[g, j - 1], where)

    def end_copy(g, j):
        to_orb, where = peer(j)
        return remote(end_parts.at[g, j % reps, pl.ds(to_orb * rows_out, rows_out), :], end_arrived.at[g, j],
                      end_send.at[g, j], end_recv.at[g, j], dict(where, aux=end_aux))

    def self_copy(j):
        to_orb, where = peer(j)
        return remote(self_parts.at[j % reps, pl.ds(to_orb * rows_out, rows_out), :], self_arrived.at[j - 1],
                      self_send.at[j - 1], self_recv.at[j - 1], where)

    def prepare(c):
        raw_copy(c).wait()
        for n in range(rows_piece // chunk):
            first = c * rows_piece + n * chunk
            span = pl.ds(first, chunk)
            turned = pltpu.einshape("ald->lad", raw[span])
            block = first // BLOCK
            weight = jnp.concatenate(
                [jnp.full((chunk, BLOCK), mask_ref[block, b].astype(F32)) for b in range(orb_cols // BLOCK)], 1
            ).astype(BF16)
            for i in range(half):
                mine = turned[i]
                for q in range(1, reps):
                    mine = jnp.where(r == q, turned[q * half + i], mine)
                masked[i, span, :] = mine * weight

    def flat_dot(block, dens):
        count = block.shape[1]
        made = jnp.dot(block.reshape(half * count, orb_cols), dens[...], preferred_element_type=F32).astype(BF16)
        return jnp.concatenate([made[i * count:(i + 1) * count] for i in range(half)], 1)

    def tile(which, block):
        moved = flat_dot(block, virt_dens)
        return lax.dot_general(occ[which], moved, CONTRACT, preferred_element_type=F32) * factor

    prepare(0)
    pl.semaphore_wait(
        barrier,
        peers + jnp.where(inner, chips - 1, chips - 2)
        + jnp.where(jnp.logical_or(feeds, at_end), peers - 1, 0),
    )
    for c in range(pieces):
        if c > 0:
            prepare(c)
        sends(c, 1, False)

        @pl.when(inner)
        def _():
            cross(c, z, piece(c)).start()
            local(c).start()
    for d in range(2, chips - 1):
        for c in range(pieces):
            sends(c, d, False)

    occ_copy.wait()
    virt_copy.wait()
    for c in range(pieces):
        occ[0, rows(c), :] = flat_dot(masked[:, rows(c), :], occ_dens)
    for s in reversed(range(reps)):
        side = (r + s) % reps
        total = tile(0, masked[:, pl.ds(side * self_cols, self_cols), :])
        self_parts[s] = total.astype(BF16)
        if s == 0:
            self_whole[...] = total
        for j in range(1, peers):
            if j % reps == s:
                self_copy(j).start()

    for d in range(1, chips - 2):
        for c in range(pieces):
            arrive(c, d)
            if d == 1:
                @pl.when(feeds)
                def _():
                    rows_e = gath[c // per_group][end_aux, :, pl.ds(c % per_group * rows_piece, rows_piece), :]
                    occ[1, rows(c), :] = flat_dot(rows_e, occ_dens)

    def group(g):
        span = range(g * per_group, (g + 1) * per_group)
        for c in span:
            arrive(c, chips - 2)

        @pl.when(inner)
        def _():
            for c in span:
                for zz in range(chips):
                    cross(c, zz, slot(c, 2 * zz + 1 - k)).wait_recv()
                local(c).wait()

            @pl.when(feeds)
            def _():
                for s in reversed(range(reps)):
                    partner = match_ref[(r + s) % reps, end_aux]
                    end_parts[g, s] = tile(1, gath[g][partner]).astype(BF16)
                    for j in range(peers):
                        if j % reps == s:
                            end_copy(g, j).start()

            for s in reversed(range(reps)):
                partner = match_ref[(r + s) % reps, a]
                total = tile(0, gath[g][partner])
                parts[g, s] = total.astype(BF16)
                if s == 0:
                    whole[g] = total
                for j in range(1, peers):
                    if j % reps == s:
                        part_copy(g, j).start()

    def finish(g):
        @pl.when(inner)
        def _():
            total = whole[g, pl.ds(o * rows_out, rows_out), :]
            for j in range(1, peers):
                part_copy(g, j).wait_recv()
                total = total + arrived[g, j - 1].astype(F32)
            pair_out[:, g * cols_group:(g + 1) * cols_group] = total

    def finish_end(g):
        @pl.when(at_end)
        def _():
            total = None
            for j in range(peers):
                end_copy(g, j).wait_recv()
                term = end_arrived[g, j].astype(F32)
                total = term if total is None else total + term
            pair_out[:, g * cols_group:(g + 1) * cols_group] = total

    def finish_self():
        total = self_whole[pl.ds(o * rows_out, rows_out), :]
        for j in range(1, peers):
            self_copy(j).wait_recv()
            total = total + self_arrived[j - 1].astype(F32)
        self_out[...] = total

    finish_self()
    for g in range(groups):
        group(g)
        if g > 0:
            finish(g - 1)
        finish_end(g)
    finish(groups - 1)

    for c in range(pieces):
        for d in range(1, chips - 1):
            sends(c, d, True)

        @pl.when(inner)
        def _():
            for zz in range(chips):
                cross(c, zz, piece(c)).wait_send()
    for j in range(1, peers):
        self_copy(j).wait_send()
    for g in range(groups):
        @pl.when(inner)
        def _():
            for j in range(1, peers):
                part_copy(g, j).wait_send()

        @pl.when(feeds)
        def _():
            for j in range(peers):
                end_copy(g, j).wait_send()


def per_device(slab, occ_density, virt_density, block_mask, matching):
    owners = lax.axis_size("aux")
    orbs = lax.axis_size("orb")
    reps = lax.axis_size("rep")
    chips = owners // 2
    aux_rows, batch, orb_cols = slab.shape
    pieces = max(2, 32 // chips)
    rows_piece = aux_rows // pieces
    per_group = max(1, BLOCK // rows_piece)
    groups = pieces // per_group
    cols_group = per_group * rows_piece
    half = batch // reps
    rows_out = aux_rows // orbs
    self_cols = aux_rows // reps
    peers = orbs * reps
    chunk = min(rows_piece, BLOCK // 2)
    factor = 1.0 / math.sqrt(batch * orb_cols * orbs)
    dma = pltpu.SemaphoreType.DMA
    vmem = pl.BlockSpec(memory_space=pltpu.VMEM)
    smem = pl.BlockSpec(memory_space=pltpu.SMEM)
    hbm = pl.BlockSpec(memory_space=pltpu.HBM)
    buffers = [((owners, half, cols_group, orb_cols), BF16) for _ in range(groups)] + [
        ((aux_rows, batch, orb_cols), BF16),
        ((half, aux_rows, orb_cols), BF16),
        ((orb_cols, orb_cols), BF16),
        ((orb_cols, orb_cols), BF16),
        ((2, aux_rows, half * orb_cols), BF16),
        ((groups, reps, aux_rows, cols_group), BF16),
        ((groups, reps, aux_rows, cols_group), BF16),
        ((groups, aux_rows, cols_group), F32),
        ((groups, peers - 1, rows_out, cols_group), BF16),
        ((groups, peers, rows_out, cols_group), BF16),
        ((reps, aux_rows, self_cols), BF16),
        ((aux_rows, self_cols), F32),
        ((peers - 1, rows_out, self_cols), BF16),
    ]
    held = sum(math.prod(shape) * jnp.dtype(kind).itemsize for shape, kind in buffers)
    pair, own = pl.pallas_call(
        functools.partial(kernel, (chips, orbs, reps, pieces, groups, chunk), factor),
        out_shape=(
            jax.ShapeDtypeStruct((rows_out, aux_rows), F32),
            jax.ShapeDtypeStruct((rows_out, self_cols), F32),
        ),
        in_specs=[smem, smem, hbm, hbm, hbm],
        out_specs=(vmem, vmem),
        scratch_shapes=[pltpu.VMEM(shape, kind) for shape, kind in buffers] + [
            dma((pieces,)), dma((2,)), dma((pieces,)),
            dma((pieces, chips)), dma((pieces, chips)), dma((pieces, chips)), dma((pieces, chips)),
            dma((groups, peers - 1)), dma((groups, peers - 1)),
            dma((groups, peers)), dma((groups, peers)),
            dma((peers - 1,)), dma((peers - 1,)),
        ],
        compiler_params=pltpu.CompilerParams(
            collective_id=0, has_side_effects=True, vmem_limit_bytes=held + 8 * 2**20
        ),
    )(matching, block_mask, slab, occ_density, virt_density)
    return (pair[None], own)


def solution(mesh):
    return jax.shard_map(
        per_device,
        mesh=mesh,
        in_specs=(P("aux", None, "orb"), P("orb", None), P("orb", None), P("aux", "orb"), P()),
        out_specs=(P("rep", ("aux", "orb"), None), P(("aux", "orb"), "rep")),
        check_vma=False,
    )
```

```python
import functools
import math

import jax
import jax.numpy as jnp
from jax import lax
from jax.experimental import pallas as pl
from jax.experimental.pallas import tpu as pltpu
from jax.sharding import PartitionSpec as P

BLOCK = 128
MESH = pl.DeviceIdType.MESH
CONTRACT = (((1,), (1,)), ((), ()))
F32, BF16 = jnp.float32, jnp.bfloat16


def kernel(sizes, factor, match_hbm, mask_hbm, slab, occ_hbm, virt_hbm, pair_out, self_out, *scratch):
    chips, orbs, reps, pieces, groups, chunk = sizes
    gath = scratch[:groups]
    (match_ref, mask_ref, raw, masked, occ_dens, virt_dens, occ, parts, end_parts, whole, arrived, end_arrived,
     self_parts, self_whole, self_arrived, small_sem, raw_sem, dens_sem, local_sem, up_sem, down_sem,
     recv_sem, core_send, core_recv, part_send, part_recv, end_send, end_recv, self_send, self_recv) = scratch[groups:]
    half, aux_rows, orb_cols = masked.shape
    rows_piece = aux_rows // pieces
    per_group = pieces // groups
    cols_group = aux_rows // groups
    rows_out = aux_rows // orbs
    self_cols = aux_rows // reps
    peers = orbs * reps

    a = lax.axis_index("aux")
    o = lax.axis_index("orb")
    r = lax.axis_index("rep")
    z = a // 2
    k = a % 2
    inner = jnp.logical_and(z >= 1, z <= chips - 2)
    at_end = jnp.logical_not(inner)
    feeds = jnp.logical_or(z == 1, z == chips - 2)
    end_aux = jnp.where(z == 1, k, 2 * (chips - 1) + k)
    feed_aux = jnp.where(z == 0, 2 + k, 2 * (chips - 2) + k)
    other = 2 * z + 1 - k
    up_ok = z + 1 <= chips - 2
    down_ok = z - 1 >= 1

    def peer(j):
        to_orb, to_rep = (o + j // reps) % orbs, (r + j % reps) % reps
        return to_orb, {"orb": to_orb, "rep": to_rep}

    def rows(c):
        return pl.ds(c * rows_piece, rows_piece)

    def raw_copy(c):
        return pltpu.make_async_copy(slab.at[rows(c)], raw.at[rows(c)], raw_sem.at[c])

    mask_copy = pltpu.make_async_copy(mask_hbm, mask_ref, small_sem.at[0])
    match_copy = pltpu.make_async_copy(match_hbm, match_ref, small_sem.at[1])
    mask_copy.start()
    for c in range(pieces):
        raw_copy(c).start()
    match_copy.start()
    occ_copy = pltpu.make_async_copy(occ_hbm, occ_dens, dens_sem.at[0])
    virt_copy = pltpu.make_async_copy(virt_hbm, virt_dens, dens_sem.at[1])
    occ_copy.start()
    virt_copy.start()

    barrier = pltpu.get_barrier_semaphore()

    def greet(where):
        pl.semaphore_signal(barrier, inc=1, device_id=where, device_id_type=MESH)

    @pl.when(z > 0)
    def _():
        greet({"aux": a - 2})

    @pl.when(z < chips - 1)
    def _():
        greet({"aux": a + 2})

    greet({"aux": other})
    for j in range(1, peers):
        greet(peer(j)[1])

        @pl.when(feeds)
        def _():
            greet(dict(peer(j)[1], aux=end_aux))

        @pl.when(at_end)
        def _():
            greet(dict(peer(j)[1], aux=feed_aux))

    def remote(src, dst, send, recv, where):
        return pltpu.make_async_remote_copy(
            src_ref=src, dst_ref=dst, send_sem=send, recv_sem=recv, device_id=where, device_id_type=MESH
        )

    def piece(c):
        return masked.at[:, rows(c), :]

    def slot(c, owner):
        return gath[c // per_group].at[owner, :, pl.ds(c % per_group * rows_piece, rows_piece), :]

    def up(c, zz, src):
        return remote(src, slot(c, 2 * zz + k), up_sem.at[c, zz], recv_sem.at[c, zz], {"aux": a + 2})

    def down(c, zz, src):
        return remote(src, slot(c, 2 * zz + k), down_sem.at[c, zz], recv_sem.at[c, zz], {"aux": a - 2})

    def cross(c, zz, src):
        return remote(src, slot(c, 2 * zz + k), core_send.at[c, zz], core_recv.at[c, zz], {"aux": other})

    def local(c):
        return pltpu.make_async_copy(piece(c), slot(c, a), local_sem.at[c])

    def lower(c, send):
        for d in range(1, chips):
            @pl.when(z - d >= 0)
            def _():
                zz = jnp.maximum(z - d, 0)
                up(c, zz, slot(c, 2 * zz + k)).wait_recv()
                if send:
                    up(c, zz, slot(c, 2 * zz + k)).start()
                cross(c, zz, slot(c, 2 * zz + k)).start()

    def upper(c, send):
        for d in range(1, chips):
            @pl.when(z + d <= chips - 1)
            def _():
                zz = jnp.minimum(z + d, chips - 1)
                down(c, zz, slot(c, 2 * zz + k)).wait_recv()
                if send:
                    down(c, zz, slot(c, 2 * zz + k)).start()
                cross(c, zz, slot(c, 2 * zz + k)).start()

    def own(c):
        @pl.when(up_ok)
        def _():
            up(c, z, piece(c)).start()

        @pl.when(down_ok)
        def _():
            down(c, z, piece(c)).start()

    def relay(c):
        @pl.when(jnp.logical_and(inner, up_ok))
        def _():
            lower(c, True)

        @pl.when(jnp.logical_and(inner, down_ok))
        def _():
            upper(c, True)

        @pl.when(feeds)
        def _():
            rows_e = gath[c // per_group][end_aux, :, pl.ds(c % per_group * rows_piece, rows_piece), :]
            occ[1, rows(c), :] = flat_dot(rows_e, occ_dens)

    def complete(c):
        @pl.when(inner)
        def _():
            @pl.when(jnp.logical_not(up_ok))
            def _():
                lower(c, False)

            @pl.when(jnp.logical_not(down_ok))
            def _():
                upper(c, False)

    def part_copy(g, j):
        to_orb, where = peer(j)
        return remote(parts.at[g, j % reps, pl.ds(to_orb * rows_out, rows_out), :], arrived.at[g, j - 1],
                      part_send.at[g, j - 1], part_recv.at[g, j - 1], where)

    def end_copy(g, j):
        to_orb, where = peer(j)
        return remote(end_parts.at[g, j % reps, pl.ds(to_orb * rows_out, rows_out), :], end_arrived.at[g, j],
                      end_send.at[g, j], end_recv.at[g, j], dict(where, aux=end_aux))

    def self_copy(j):
        to_orb, where = peer(j)
        return remote(self_parts.at[j % reps, pl.ds(to_orb * rows_out, rows_out), :], self_arrived.at[j - 1],
                      self_send.at[j - 1], self_recv.at[j - 1], where)

    def prepare(c):
        raw_copy(c).wait()
        for n in range(rows_piece // chunk):
            first = c * rows_piece + n * chunk
            span = pl.ds(first, chunk)
            turned = pltpu.einshape("ald->lad", raw[span])
            block = first // BLOCK
            weight = jnp.concatenate(
                [jnp.full((chunk, BLOCK), mask_ref[block, b].astype(F32)) for b in range(orb_cols // BLOCK)], 1
            ).astype(BF16)
            for i in range(half):
                mine = turned[i]
                for q in range(1, reps):
                    mine = jnp.where(r == q, turned[q * half + i], mine)
                masked[i, span, :] = mine * weight

    def flat_dot(block, dens):
        count = block.shape[1]
        made = jnp.dot(block.reshape(half * count, orb_cols), dens[...], preferred_element_type=F32).astype(BF16)
        return jnp.concatenate([made[i * count:(i + 1) * count] for i in range(half)], 1)

    def tile(which, block):
        moved = flat_dot(block, virt_dens)
        return lax.dot_general(occ[which], moved, CONTRACT, preferred_element_type=F32) * factor

    def gathered(g):
        @pl.when(inner)
        def _():
            for c in range(g * per_group, (g + 1) * per_group):
                for zz in range(chips):
                    cross(c, zz, slot(c, 2 * zz + 1 - k)).wait_recv()
                local(c).wait()

    def end_tiles(g):
        @pl.when(feeds)
        def _():
            for s in reversed(range(reps)):
                partner = match_ref[(r + s) % reps, end_aux]
                end_parts[g, s] = tile(1, gath[g][partner]).astype(BF16)
                for j in range(peers):
                    if j % reps == s:
                        end_copy(g, j).start()

    def own_tiles(g):
        @pl.when(inner)
        def _():
            for s in reversed(range(reps)):
                partner = match_ref[(r + s) % reps, a]
                total = tile(0, gath[g][partner])
                parts[g, s] = total.astype(BF16)
                if s == 0:
                    whole[g] = total
                for j in range(1, peers):
                    if j % reps == s:
                        part_copy(g, j).start()

    def self_tiles():
        for s in reversed(range(reps)):
            side = (r + s) % reps
            total = tile(0, masked[:, pl.ds(side * self_cols, self_cols), :])
            self_parts[s] = total.astype(BF16)
            if s == 0:
                self_whole[...] = total
            for j in range(1, peers):
                if j % reps == s:
                    self_copy(j).start()

    def finish(g):
        @pl.when(inner)
        def _():
            total = whole[g, pl.ds(o * rows_out, rows_out), :]
            for j in range(1, peers):
                part_copy(g, j).wait_recv()
                total = total + arrived[g, j - 1].astype(F32)
            pair_out[:, g * cols_group:(g + 1) * cols_group] = total

    def finish_end(g):
        @pl.when(at_end)
        def _():
            total = None
            for j in range(peers):
                end_copy(g, j).wait_recv()
                term = end_arrived[g, j].astype(F32)
                total = term if total is None else total + term
            pair_out[:, g * cols_group:(g + 1) * cols_group] = total

    def finish_self():
        total = self_whole[pl.ds(o * rows_out, rows_out), :]
        for j in range(1, peers):
            self_copy(j).wait_recv()
            total = total + self_arrived[j - 1].astype(F32)
        self_out[...] = total

    mask_copy.wait()
    for c in range(pieces):
        prepare(c)
        if c == 0:
            pl.semaphore_wait(
                barrier,
                peers + jnp.where(inner, 2, 1) + jnp.where(jnp.logical_or(feeds, at_end), peers - 1, 0),
            )
        if c < 2:
            own(c)

        @pl.when(inner)
        def _():
            cross(c, z, piece(c)).start()
            local(c).start()

    match_copy.wait()
    occ_copy.wait()
    virt_copy.wait()
    for c in range(pieces):
        occ[0, rows(c), :] = flat_dot(masked[:, rows(c), :], occ_dens)
    ahead = min(3, pieces)
    for c in range(ahead):
        relay(c)
        if c == 0:
            self_tiles()
    made = ended = closed = 0
    for c in range(pieces):
        if c + 2 < pieces:
            own(c + 2)
        if c + ahead < pieces:
            relay(c + ahead)
        complete(c)
        if (c + 1) % per_group == 0:
            g = c // per_group
            gathered(g)
            if c + ahead >= pieces - 1:
                for e in range(ended, g + 1):
                    end_tiles(e)
                ended = g + 1
            own_tiles(g)
            if g == 0:
                finish_self()
            else:
                finish(g - 1)
    finish(groups - 1)
    for g in range(groups):
        finish_end(g)

    for c in range(pieces):
        for d in range(chips):
            @pl.when(jnp.logical_and(up_ok, z - d >= 0))
            def _():
                up(c, jnp.maximum(z - d, 0), piece(c)).wait_send()

            @pl.when(jnp.logical_and(down_ok, z + d <= chips - 1))
            def _():
                down(c, jnp.minimum(z + d, chips - 1), piece(c)).wait_send()

        @pl.when(inner)
        def _():
            for zz in range(chips):
                cross(c, zz, piece(c)).wait_send()
    for j in range(1, peers):
        self_copy(j).wait_send()
    for g in range(groups):
        @pl.when(inner)
        def _():
            for j in range(1, peers):
                part_copy(g, j).wait_send()

        @pl.when(feeds)
        def _():
            for j in range(peers):
                end_copy(g, j).wait_send()


def per_device(slab, occ_density, virt_density, block_mask, matching):
    owners = lax.axis_size("aux")
    orbs = lax.axis_size("orb")
    reps = lax.axis_size("rep")
    chips = owners // 2
    aux_rows, batch, orb_cols = slab.shape
    pieces = max(2, 32 // chips)
    rows_piece = aux_rows // pieces
    per_group = max(1, BLOCK // rows_piece)
    groups = pieces // per_group
    cols_group = per_group * rows_piece
    half = batch // reps
    rows_out = aux_rows // orbs
    self_cols = aux_rows // reps
    peers = orbs * reps
    chunk = min(rows_piece, BLOCK // 2)
    factor = 1.0 / math.sqrt(batch * orb_cols * orbs)
    dma = pltpu.SemaphoreType.DMA
    vmem = pl.BlockSpec(memory_space=pltpu.VMEM)
    hbm = pl.BlockSpec(memory_space=pltpu.HBM)
    gathers = [pltpu.VMEM((owners, half, cols_group, orb_cols), BF16) for _ in range(groups)]
    buffers = [
        ((aux_rows, batch, orb_cols), BF16),
        ((half, aux_rows, orb_cols), BF16),
        ((orb_cols, orb_cols), BF16),
        ((orb_cols, orb_cols), BF16),
        ((2, aux_rows, half * orb_cols), BF16),
        ((groups, reps, aux_rows, cols_group), BF16),
        ((groups, reps, aux_rows, cols_group), BF16),
        ((groups, aux_rows, cols_group), F32),
        ((groups, peers - 1, rows_out, cols_group), BF16),
        ((groups, peers, rows_out, cols_group), BF16),
        ((reps, aux_rows, self_cols), BF16),
        ((aux_rows, self_cols), F32),
        ((peers - 1, rows_out, self_cols), BF16),
    ]
    held = sum(math.prod(shape) * jnp.dtype(kind).itemsize for shape, kind in buffers)
    held += owners * half * aux_rows * orb_cols * jnp.dtype(BF16).itemsize
    pair, own = pl.pallas_call(
        functools.partial(kernel, (chips, orbs, reps, pieces, groups, chunk), factor),
        out_shape=(
            jax.ShapeDtypeStruct((rows_out, aux_rows), F32),
            jax.ShapeDtypeStruct((rows_out, self_cols), F32),
        ),
        in_specs=[hbm] * 5,
        out_specs=(vmem, vmem),
        scratch_shapes=gathers + [
            pltpu.SMEM(matching.shape, matching.dtype), pltpu.SMEM(block_mask.shape, block_mask.dtype),
        ] + [pltpu.VMEM(shape, kind) for shape, kind in buffers] + [
            dma((2,)), dma((pieces,)), dma((2,)), dma((pieces,)), dma((pieces, chips)),
            dma((pieces, chips)), dma((pieces, chips)), dma((pieces, chips)), dma((pieces, chips)),
            dma((groups, peers - 1)), dma((groups, peers - 1)),
            dma((groups, peers)), dma((groups, peers)),
            dma((peers - 1,)), dma((peers - 1,)),
        ],
        compiler_params=pltpu.CompilerParams(
            collective_id=0, has_side_effects=True, vmem_limit_bytes=held + 8 * 2**20
        ),
    )(*(pltpu.with_memory_space_constraint(x, pltpu.HBM)
        for x in (matching, block_mask, slab, occ_density, virt_density)))
    return (pair[None], own)


def solution(mesh):
    return jax.shard_map(
        per_device,
        mesh=mesh,
        in_specs=(P("aux", None, "orb"), P("orb", None), P("orb", None), P("aux", "orb"), P()),
        out_specs=(P("rep", ("aux", "orb"), None), P(("aux", "orb"), "rep")),
        check_vma=False,
    )
```

```python
import functools
import math

import jax
import jax.numpy as jnp
from jax import lax
from jax.experimental import pallas as pl
from jax.experimental.pallas import tpu as pltpu
from jax.sharding import PartitionSpec as P

BLOCK = 128
MESH = pl.DeviceIdType.MESH
CONTRACT = (((1,), (1,)), ((), ()))
F32, BF16 = jnp.float32, jnp.bfloat16


def kernel(sizes, factor, match_hbm, mask_hbm, slab, occ_hbm, virt_hbm, pair_out, self_out, *scratch):
    chips, orbs, reps, pieces, chunk = sizes
    gath = scratch[:pieces]
    (match_ref, mask_ref, raw, masked, occ_dens, virt_dens, occ, parts, end_parts, whole, arrived, end_arrived,
     self_parts, self_whole, self_arrived, small_sem, raw_sem, dens_sem, local_sem, up_sem, down_sem,
     recv_sem, core_send, core_recv, part_send, part_recv, end_send, end_recv, self_send, self_recv) = scratch[pieces:]
    half, aux_rows, orb_cols = masked.shape
    rows_piece = aux_rows // pieces
    rows_out = aux_rows // orbs
    self_cols = aux_rows // reps
    peers = orbs * reps

    a = lax.axis_index("aux")
    o = lax.axis_index("orb")
    r = lax.axis_index("rep")
    z = a // 2
    k = a % 2
    inner = jnp.logical_and(z >= 1, z <= chips - 2)
    at_end = jnp.logical_not(inner)
    feeds = jnp.logical_or(z == 1, z == chips - 2)
    end_aux = jnp.where(z == 1, k, 2 * (chips - 1) + k)
    feed_aux = jnp.where(z == 0, 2 + k, 2 * (chips - 2) + k)
    other = 2 * z + 1 - k
    up_ok = z + 1 <= chips - 2
    down_ok = z - 1 >= 1

    def peer(j):
        to_orb, to_rep = (o + j // reps) % orbs, (r + j % reps) % reps
        return to_orb, {"orb": to_orb, "rep": to_rep}

    def rows(c):
        return pl.ds(c * rows_piece, rows_piece)

    def raw_copy(c):
        return pltpu.make_async_copy(slab.at[rows(c)], raw.at[rows(c)], raw_sem.at[c])

    mask_copy = pltpu.make_async_copy(mask_hbm, mask_ref, small_sem.at[0])
    match_copy = pltpu.make_async_copy(match_hbm, match_ref, small_sem.at[1])
    mask_copy.start()
    for c in range(pieces):
        raw_copy(c).start()
    match_copy.start()
    occ_copy = pltpu.make_async_copy(occ_hbm, occ_dens, dens_sem.at[0])
    virt_copy = pltpu.make_async_copy(virt_hbm, virt_dens, dens_sem.at[1])
    occ_copy.start()
    virt_copy.start()

    barrier = pltpu.get_barrier_semaphore()

    def greet(where):
        pl.semaphore_signal(barrier, inc=1, device_id=where, device_id_type=MESH)

    @pl.when(z > 0)
    def _():
        greet({"aux": a - 2})

    @pl.when(z < chips - 1)
    def _():
        greet({"aux": a + 2})

    greet({"aux": other})
    for j in range(1, peers):
        greet(peer(j)[1])

        @pl.when(feeds)
        def _():
            greet(dict(peer(j)[1], aux=end_aux))

        @pl.when(at_end)
        def _():
            greet(dict(peer(j)[1], aux=feed_aux))

    def remote(src, dst, send, recv, where):
        return pltpu.make_async_remote_copy(
            src_ref=src, dst_ref=dst, send_sem=send, recv_sem=recv, device_id=where, device_id_type=MESH
        )

    def piece(c):
        return masked.at[:, rows(c), :]

    def slot(c, owner):
        return gath[c].at[owner]

    def up(c, zz, src):
        return remote(src, slot(c, 2 * zz + k), up_sem.at[c, zz], recv_sem.at[c, zz], {"aux": a + 2})

    def down(c, zz, src):
        return remote(src, slot(c, 2 * zz + k), down_sem.at[c, zz], recv_sem.at[c, zz], {"aux": a - 2})

    def cross(c, zz, src):
        return remote(src, slot(c, 2 * zz + k), core_send.at[c, zz], core_recv.at[c, zz], {"aux": other})

    def local(c):
        return pltpu.make_async_copy(piece(c), slot(c, a), local_sem.at[c])

    def lower(c, send):
        for d in range(1, chips):
            @pl.when(z - d >= 0)
            def _():
                zz = jnp.maximum(z - d, 0)
                up(c, zz, slot(c, 2 * zz + k)).wait_recv()
                if send:
                    up(c, zz, slot(c, 2 * zz + k)).start()
                cross(c, zz, slot(c, 2 * zz + k)).start()

    def upper(c, send):
        for d in range(1, chips):
            @pl.when(z + d <= chips - 1)
            def _():
                zz = jnp.minimum(z + d, chips - 1)
                down(c, zz, slot(c, 2 * zz + k)).wait_recv()
                if send:
                    down(c, zz, slot(c, 2 * zz + k)).start()
                cross(c, zz, slot(c, 2 * zz + k)).start()

    def own(c):
        @pl.when(up_ok)
        def _():
            up(c, z, piece(c)).start()

        @pl.when(down_ok)
        def _():
            down(c, z, piece(c)).start()

    def relay(c):
        @pl.when(jnp.logical_and(inner, up_ok))
        def _():
            lower(c, True)

        @pl.when(jnp.logical_and(inner, down_ok))
        def _():
            upper(c, True)

        @pl.when(feeds)
        def _():
            occ[1, rows(c), :] = flat_dot(gath[c][end_aux], occ_dens)

    def complete(c):
        @pl.when(inner)
        def _():
            @pl.when(jnp.logical_not(up_ok))
            def _():
                lower(c, False)

            @pl.when(jnp.logical_not(down_ok))
            def _():
                upper(c, False)

    def part_copy(c, j):
        to_orb, where = peer(j)
        return remote(parts.at[c, j % reps, to_orb], arrived.at[c, j - 1],
                      part_send.at[c, j - 1], part_recv.at[c, j - 1], where)

    def end_copy(c, j):
        to_orb, where = peer(j)
        return remote(end_parts.at[c, j % reps, to_orb], end_arrived.at[c, j],
                      end_send.at[c, j], end_recv.at[c, j], dict(where, aux=end_aux))

    def self_copy(j):
        to_orb, where = peer(j)
        return remote(self_parts.at[j % reps, pl.ds(to_orb * rows_out, rows_out), :], self_arrived.at[j - 1],
                      self_send.at[j - 1], self_recv.at[j - 1], where)

    def prepare(c):
        raw_copy(c).wait()
        for n in range(rows_piece // chunk):
            first = c * rows_piece + n * chunk
            span = pl.ds(first, chunk)
            turned = pltpu.einshape("ald->lad", raw[span])
            block = first // BLOCK
            weight = jnp.concatenate(
                [jnp.full((chunk, BLOCK), mask_ref[block, b].astype(F32)) for b in range(orb_cols // BLOCK)], 1
            ).astype(BF16)
            for i in range(half):
                mine = turned[i]
                for q in range(1, reps):
                    mine = jnp.where(r == q, turned[q * half + i], mine)
                masked[i, span, :] = mine * weight

    def flat_dot(block, dens):
        count = block.shape[1]
        made = jnp.dot(block.reshape(half * count, orb_cols), dens[...], preferred_element_type=F32).astype(BF16)
        return jnp.concatenate([made[i * count:(i + 1) * count] for i in range(half)], 1)

    def self_tile(block):
        moved = flat_dot(block, virt_dens)
        return lax.dot_general(occ[0], moved, CONTRACT, preferred_element_type=F32) * factor

    def turned_tiles(c, which, owner):
        blocks = jnp.concatenate([gath[c][match_ref[(r + s) % reps, owner]] for s in range(reps)], 1)
        moved = flat_dot(blocks, virt_dens)
        total = lax.dot_general(moved, occ[which], CONTRACT, preferred_element_type=F32) * factor
        return [[total[s * rows_piece:(s + 1) * rows_piece, q * rows_out:(q + 1) * rows_out]
                 for q in range(orbs)] for s in range(reps)]

    def gathered(c):
        @pl.when(inner)
        def _():
            for zz in range(chips):
                cross(c, zz, slot(c, 2 * zz + 1 - k)).wait_recv()
            local(c).wait()

    def end_tiles(c):
        @pl.when(feeds)
        def _():
            tiles = turned_tiles(c, 1, end_aux)
            for s in reversed(range(reps)):
                for q in range(orbs):
                    end_parts[c, s, q] = tiles[s][q].astype(BF16)
            for j in reversed(range(peers)):
                end_copy(c, j).start()

    def own_tiles(c):
        @pl.when(inner)
        def _():
            tiles = turned_tiles(c, 0, a)
            for s in reversed(range(reps)):
                for q in range(orbs):
                    parts[c, s, q] = tiles[s][q].astype(BF16)
                    if s == 0:
                        whole[c, q] = tiles[s][q]
            for j in reversed(range(1, peers)):
                part_copy(c, j).start()

    def self_tiles():
        for s in reversed(range(reps)):
            side = (r + s) % reps
            total = self_tile(masked[:, pl.ds(side * self_cols, self_cols), :])
            self_parts[s] = total.astype(BF16)
            if s == 0:
                self_whole[...] = total
            for j in range(1, peers):
                if j % reps == s:
                    self_copy(j).start()

    def columns(c):
        return slice(c * rows_piece, (c + 1) * rows_piece)

    def finish(c):
        @pl.when(inner)
        def _():
            total = whole[c, o]
            for j in range(1, peers):
                part_copy(c, j).wait_recv()
                total = total + arrived[c, j - 1].astype(F32)
            pair_out[:, columns(c)] = total.T

    def finish_end(c):
        @pl.when(at_end)
        def _():
            total = None
            for j in range(peers):
                end_copy(c, j).wait_recv()
                term = end_arrived[c, j].astype(F32)
                total = term if total is None else total + term
            pair_out[:, columns(c)] = total.T

    def finish_self():
        total = self_whole[pl.ds(o * rows_out, rows_out), :]
        for j in range(1, peers):
            self_copy(j).wait_recv()
            total = total + self_arrived[j - 1].astype(F32)
        self_out[...] = total

    mask_copy.wait()
    for c in range(pieces):
        prepare(c)
        if c == 0:
            pl.semaphore_wait(
                barrier,
                peers + jnp.where(inner, 2, 1) + jnp.where(jnp.logical_or(feeds, at_end), peers - 1, 0),
            )
        if c < 2:
            own(c)

        @pl.when(inner)
        def _():
            cross(c, z, piece(c)).start()
            local(c).start()

    match_copy.wait()
    occ_copy.wait()
    virt_copy.wait()
    for c in range(pieces):
        occ[0, rows(c), :] = flat_dot(masked[:, rows(c), :], occ_dens)
    ahead = min(3, pieces)
    for c in range(ahead):
        relay(c)
        if c == 0:
            self_tiles()
    ended = 0
    lag = 2
    for c in range(pieces):
        if c + 2 < pieces:
            own(c + 2)
        if c + ahead < pieces:
            relay(c + ahead)
        filled = c + ahead >= pieces - 1
        while filled and ended < c:
            end_tiles(ended)
            ended += 1
        complete(c)
        gathered(c)
        if filled:
            end_tiles(c)
            ended += 1
        own_tiles(c)
        if c == 0:
            finish_self()
        if c >= lag:
            finish(c - lag)
    for c in range(max(0, pieces - lag), pieces):
        finish(c)
    for c in range(pieces):
        finish_end(c)

    for c in range(pieces):
        for d in range(chips):
            @pl.when(jnp.logical_and(up_ok, z - d >= 0))
            def _():
                up(c, jnp.maximum(z - d, 0), piece(c)).wait_send()

            @pl.when(jnp.logical_and(down_ok, z + d <= chips - 1))
            def _():
                down(c, jnp.minimum(z + d, chips - 1), piece(c)).wait_send()

        @pl.when(inner)
        def _():
            for zz in range(chips):
                cross(c, zz, piece(c)).wait_send()
    for j in range(1, peers):
        self_copy(j).wait_send()
    for c in range(pieces):
        @pl.when(inner)
        def _():
            for j in range(1, peers):
                part_copy(c, j).wait_send()

        @pl.when(feeds)
        def _():
            for j in range(peers):
                end_copy(c, j).wait_send()


def per_device(slab, occ_density, virt_density, block_mask, matching):
    owners = lax.axis_size("aux")
    orbs = lax.axis_size("orb")
    reps = lax.axis_size("rep")
    chips = owners // 2
    aux_rows, batch, orb_cols = slab.shape
    pieces = max(2, 32 // chips)
    rows_piece = aux_rows // pieces
    half = batch // reps
    rows_out = aux_rows // orbs
    self_cols = aux_rows // reps
    peers = orbs * reps
    chunk = min(rows_piece, BLOCK // 2)
    factor = 1.0 / math.sqrt(batch * orb_cols * orbs)
    dma = pltpu.SemaphoreType.DMA
    vmem = pl.BlockSpec(memory_space=pltpu.VMEM)
    hbm = pl.BlockSpec(memory_space=pltpu.HBM)
    gathers = [pltpu.VMEM((owners, half, rows_piece, orb_cols), BF16) for _ in range(pieces)]
    buffers = [
        ((aux_rows, batch, orb_cols), BF16),
        ((half, aux_rows, orb_cols), BF16),
        ((orb_cols, orb_cols), BF16),
        ((orb_cols, orb_cols), BF16),
        ((2, aux_rows, half * orb_cols), BF16),
        ((pieces, reps, orbs, rows_piece, rows_out), BF16),
        ((pieces, reps, orbs, rows_piece, rows_out), BF16),
        ((pieces, orbs, rows_piece, rows_out), F32),
        ((pieces, peers - 1, rows_piece, rows_out), BF16),
        ((pieces, peers, rows_piece, rows_out), BF16),
        ((reps, aux_rows, self_cols), BF16),
        ((aux_rows, self_cols), F32),
        ((peers - 1, rows_out, self_cols), BF16),
    ]
    held = sum(math.prod(shape) * jnp.dtype(kind).itemsize for shape, kind in buffers)
    held += owners * half * aux_rows * orb_cols * jnp.dtype(BF16).itemsize
    pair, own = pl.pallas_call(
        functools.partial(kernel, (chips, orbs, reps, pieces, chunk), factor),
        out_shape=(
            jax.ShapeDtypeStruct((rows_out, aux_rows), F32),
            jax.ShapeDtypeStruct((rows_out, self_cols), F32),
        ),
        in_specs=[hbm] * 5,
        out_specs=(vmem, vmem),
        scratch_shapes=gathers + [
            pltpu.SMEM(matching.shape, matching.dtype), pltpu.SMEM(block_mask.shape, block_mask.dtype),
        ] + [pltpu.VMEM(shape, kind) for shape, kind in buffers] + [
            dma((2,)), dma((pieces,)), dma((2,)), dma((pieces,)), dma((pieces, chips)),
            dma((pieces, chips)), dma((pieces, chips)), dma((pieces, chips)), dma((pieces, chips)),
            dma((pieces, peers - 1)), dma((pieces, peers - 1)),
            dma((pieces, peers)), dma((pieces, peers)),
            dma((peers - 1,)), dma((peers - 1,)),
        ],
        compiler_params=pltpu.CompilerParams(
            collective_id=0, has_side_effects=True, vmem_limit_bytes=held + 8 * 2**20
        ),
    )(*(pltpu.with_memory_space_constraint(x, pltpu.HBM)
        for x in (matching, block_mask, slab, occ_density, virt_density)))
    return (pair[None], own)


def solution(mesh):
    return jax.shard_map(
        per_device,
        mesh=mesh,
        in_specs=(P("aux", None, "orb"), P("orb", None), P("orb", None), P("aux", "orb"), P()),
        out_specs=(P("rep", ("aux", "orb"), None), P(("aux", "orb"), "rep")),
        check_vma=False,
    )
```

```python
import functools
import math

import jax
import jax.numpy as jnp
from jax import lax
from jax.experimental import pallas as pl
from jax.experimental.pallas import tpu as pltpu
from jax.sharding import PartitionSpec as P

BLOCK = 128
MESH = pl.DeviceIdType.MESH
CONTRACT = (((1,), (1,)), ((), ()))
F32, BF16 = jnp.float32, jnp.bfloat16


def kernel(sizes, factor, match_hbm, mask_hbm, slab, occ_hbm, virt_hbm, pair_out, self_out, *scratch):
    chips, orbs, reps, counts = sizes
    pieces = len(counts)
    firsts = [sum(counts[:c]) for c in range(pieces)]
    gath = scratch[:pieces]
    (match_ref, mask_ref, raw, masked, occ_dens, virt_dens, occ, parts, end_parts, whole, arrived, end_arrived,
     self_parts, self_whole, self_arrived, small_sem, raw_sem, dens_sem, local_sem, up_sem, down_sem,
     recv_sem, core_send, core_recv, part_send, part_recv, end_send, end_recv, self_send, self_recv) = scratch[pieces:]
    half, aux_rows, orb_cols = masked.shape
    rows_out = aux_rows // orbs
    self_cols = aux_rows // reps
    peers = orbs * reps

    a = lax.axis_index("aux")
    o = lax.axis_index("orb")
    r = lax.axis_index("rep")
    z = a // 2
    k = a % 2
    inner = jnp.logical_and(z >= 1, z <= chips - 2)
    at_end = jnp.logical_not(inner)
    feeds = jnp.logical_or(z == 1, z == chips - 2)
    end_aux = jnp.where(z == 1, k, 2 * (chips - 1) + k)
    feed_aux = jnp.where(z == 0, 2 + k, 2 * (chips - 2) + k)
    other = 2 * z + 1 - k
    up_ok = z + 1 <= chips - 2
    down_ok = z - 1 >= 1

    def peer(j):
        to_orb, to_rep = (o + j // reps) % orbs, (r + j % reps) % reps
        return to_orb, {"orb": to_orb, "rep": to_rep}

    def rows(c):
        return pl.ds(firsts[c], counts[c])

    def raw_copy(c):
        return pltpu.make_async_copy(slab.at[rows(c)], raw.at[rows(c)], raw_sem.at[c])

    mask_copy = pltpu.make_async_copy(mask_hbm, mask_ref, small_sem.at[0])
    match_copy = pltpu.make_async_copy(match_hbm, match_ref, small_sem.at[1])
    mask_copy.start()
    for c in range(pieces):
        raw_copy(c).start()
    match_copy.start()
    occ_copy = pltpu.make_async_copy(occ_hbm, occ_dens, dens_sem.at[0])
    virt_copy = pltpu.make_async_copy(virt_hbm, virt_dens, dens_sem.at[1])
    occ_copy.start()
    virt_copy.start()

    barrier = pltpu.get_barrier_semaphore()

    def greet(where):
        pl.semaphore_signal(barrier, inc=1, device_id=where, device_id_type=MESH)

    @pl.when(z > 0)
    def _():
        greet({"aux": a - 2})

    @pl.when(z < chips - 1)
    def _():
        greet({"aux": a + 2})

    greet({"aux": other})
    for j in range(1, peers):
        greet(peer(j)[1])

        @pl.when(feeds)
        def _():
            greet(dict(peer(j)[1], aux=end_aux))

        @pl.when(at_end)
        def _():
            greet(dict(peer(j)[1], aux=feed_aux))

    def remote(src, dst, send, recv, where):
        return pltpu.make_async_remote_copy(
            src_ref=src, dst_ref=dst, send_sem=send, recv_sem=recv, device_id=where, device_id_type=MESH
        )

    def piece(c):
        return masked.at[:, rows(c), :]

    def slot(c, owner):
        return gath[c].at[owner]

    def up(c, zz, src):
        return remote(src, slot(c, 2 * zz + k), up_sem.at[c, zz], recv_sem.at[c, zz], {"aux": a + 2})

    def down(c, zz, src):
        return remote(src, slot(c, 2 * zz + k), down_sem.at[c, zz], recv_sem.at[c, zz], {"aux": a - 2})

    def cross(c, zz, src):
        return remote(src, slot(c, 2 * zz + k), core_send.at[c, zz], core_recv.at[c, zz], {"aux": other})

    def local(c):
        return pltpu.make_async_copy(piece(c), slot(c, a), local_sem.at[c])

    def lower(c, send):
        for d in range(1, chips) if send else reversed(range(1, chips)):
            @pl.when(z - d >= 0)
            def _():
                zz = jnp.maximum(z - d, 0)
                up(c, zz, slot(c, 2 * zz + k)).wait_recv()
                if send:
                    up(c, zz, slot(c, 2 * zz + k)).start()
                cross(c, zz, slot(c, 2 * zz + k)).start()

    def upper(c, send):
        for d in range(1, chips) if send else reversed(range(1, chips)):
            @pl.when(z + d <= chips - 1)
            def _():
                zz = jnp.minimum(z + d, chips - 1)
                down(c, zz, slot(c, 2 * zz + k)).wait_recv()
                if send:
                    down(c, zz, slot(c, 2 * zz + k)).start()
                cross(c, zz, slot(c, 2 * zz + k)).start()

    def own(c):
        @pl.when(up_ok)
        def _():
            up(c, z, piece(c)).start()

        @pl.when(down_ok)
        def _():
            down(c, z, piece(c)).start()

    def relay(c):
        @pl.when(jnp.logical_and(inner, up_ok))
        def _():
            lower(c, True)

        @pl.when(jnp.logical_and(inner, down_ok))
        def _():
            upper(c, True)

        @pl.when(feeds)
        def _():
            occ[1, rows(c), :] = flat_dot(gath[c][end_aux], occ_dens)

    def complete(c):
        @pl.when(inner)
        def _():
            @pl.when(jnp.logical_not(up_ok))
            def _():
                lower(c, False)

            @pl.when(jnp.logical_not(down_ok))
            def _():
                upper(c, False)

    def part_copy(c, j):
        to_orb, where = peer(j)
        return remote(parts.at[c, j % reps, to_orb, pl.ds(0, counts[c])], arrived.at[c, j - 1, pl.ds(0, counts[c])],
                      part_send.at[c, j - 1], part_recv.at[c, j - 1], where)

    def end_copy(c, j):
        to_orb, where = peer(j)
        return remote(end_parts.at[c, j % reps, to_orb, pl.ds(0, counts[c])],
                      end_arrived.at[c, j, pl.ds(0, counts[c])],
                      end_send.at[c, j], end_recv.at[c, j], dict(where, aux=end_aux))

    def self_copy(j):
        to_orb, where = peer(j)
        return remote(self_parts.at[j % reps, pl.ds(to_orb * rows_out, rows_out), :], self_arrived.at[j - 1],
                      self_send.at[j - 1], self_recv.at[j - 1], where)

    def prepare(c):
        raw_copy(c).wait()
        chunk = min(counts[c], BLOCK // 2)
        for n in range(counts[c] // chunk):
            first = firsts[c] + n * chunk
            span = pl.ds(first, chunk)
            turned = pltpu.einshape("ald->lad", raw[span])
            block = first // BLOCK
            weight = jnp.concatenate(
                [jnp.full((chunk, BLOCK), mask_ref[block, b].astype(F32)) for b in range(orb_cols // BLOCK)], 1
            ).astype(BF16)
            for i in range(half):
                mine = turned[i]
                for q in range(1, reps):
                    mine = jnp.where(r == q, turned[q * half + i], mine)
                masked[i, span, :] = mine * weight

    def flat_dot(block, dens):
        count = block.shape[1]
        made = jnp.dot(block.reshape(half * count, orb_cols), dens[...], preferred_element_type=F32).astype(BF16)
        return jnp.concatenate([made[i * count:(i + 1) * count] for i in range(half)], 1)

    def self_tile(block):
        moved = flat_dot(block, virt_dens)
        return lax.dot_general(occ[0], moved, CONTRACT, preferred_element_type=F32) * factor

    def turned_tiles(c, which, owner):
        blocks = jnp.concatenate([gath[c][match_ref[(r + s) % reps, owner]] for s in range(reps)], 1)
        moved = flat_dot(blocks, virt_dens)
        total = lax.dot_general(moved, occ[which], CONTRACT, preferred_element_type=F32) * factor
        count = counts[c]
        return [[total[s * count:(s + 1) * count, q * rows_out:(q + 1) * rows_out]
                 for q in range(orbs)] for s in range(reps)]

    def gathered(c):
        @pl.when(inner)
        def _():
            for zz in range(chips):
                cross(c, zz, slot(c, 2 * zz + 1 - k)).wait_recv()
            local(c).wait()

    def end_tiles(c):
        @pl.when(feeds)
        def _():
            tiles = turned_tiles(c, 1, end_aux)
            for s in reversed(range(reps)):
                for q in range(orbs):
                    end_parts[c, s, q, :counts[c]] = tiles[s][q].astype(BF16)
            for j in reversed(range(peers)):
                end_copy(c, j).start()

    def own_tiles(c):
        @pl.when(inner)
        def _():
            tiles = turned_tiles(c, 0, a)
            for s in reversed(range(reps)):
                for q in range(orbs):
                    parts[c, s, q, :counts[c]] = tiles[s][q].astype(BF16)
                    if s == 0:
                        whole[c, q, :counts[c]] = tiles[s][q]
            for j in reversed(range(1, peers)):
                part_copy(c, j).start()

    def self_tiles():
        for s in reversed(range(reps)):
            side = (r + s) % reps
            total = self_tile(masked[:, pl.ds(side * self_cols, self_cols), :])
            self_parts[s] = total.astype(BF16)
            if s == 0:
                self_whole[...] = total
            for j in range(1, peers):
                if j % reps == s:
                    self_copy(j).start()

    def columns(c):
        return slice(firsts[c], firsts[c] + counts[c])

    def finish(c):
        @pl.when(inner)
        def _():
            total = whole[c, o, :counts[c]]
            for j in range(1, peers):
                part_copy(c, j).wait_recv()
                total = total + arrived[c, j - 1, :counts[c]].astype(F32)
            pair_out[:, columns(c)] = total.T

    def finish_end(c):
        @pl.when(at_end)
        def _():
            total = None
            for j in range(peers):
                end_copy(c, j).wait_recv()
                term = end_arrived[c, j, :counts[c]].astype(F32)
                total = term if total is None else total + term
            pair_out[:, columns(c)] = total.T

    def finish_self():
        total = self_whole[pl.ds(o * rows_out, rows_out), :]
        for j in range(1, peers):
            self_copy(j).wait_recv()
            total = total + self_arrived[j - 1].astype(F32)
        self_out[...] = total

    mask_copy.wait()
    for c in range(pieces):
        prepare(c)
        if c == 0:
            pl.semaphore_wait(
                barrier,
                peers + jnp.where(inner, 2, 1) + jnp.where(jnp.logical_or(feeds, at_end), peers - 1, 0),
            )
        if c < 3:
            own(c)

        @pl.when(inner)
        def _():
            cross(c, z, piece(c)).start()
            local(c).start()

    match_copy.wait()
    occ_copy.wait()
    virt_copy.wait()
    for c in range(pieces):
        occ[0, rows(c), :] = flat_dot(masked[:, rows(c), :], occ_dens)
    ahead = min(3, pieces)
    for c in range(ahead):
        relay(c)
        if c == 0:
            self_tiles()
    ended = 0
    lag = 3
    for c in range(pieces):
        if c + 3 < pieces:
            own(c + 3)
        if c + ahead < pieces:
            relay(c + ahead)
        filled = c + ahead >= pieces - 1
        while filled and ended < c:
            end_tiles(ended)
            ended += 1
        complete(c)
        gathered(c)
        if filled:
            end_tiles(c)
            ended += 1
        own_tiles(c)
        if c == 0:
            finish_self()
        if c >= lag:
            finish(c - lag)
    for c in range(max(0, pieces - lag), pieces):
        finish(c)
    for c in range(pieces):
        finish_end(c)

    for c in range(pieces):
        for d in range(chips):
            @pl.when(jnp.logical_and(up_ok, z - d >= 0))
            def _():
                up(c, jnp.maximum(z - d, 0), piece(c)).wait_send()

            @pl.when(jnp.logical_and(down_ok, z + d <= chips - 1))
            def _():
                down(c, jnp.minimum(z + d, chips - 1), piece(c)).wait_send()

        @pl.when(inner)
        def _():
            for zz in range(chips):
                cross(c, zz, piece(c)).wait_send()
    for j in range(1, peers):
        self_copy(j).wait_send()
    for c in range(pieces):
        @pl.when(inner)
        def _():
            for j in range(1, peers):
                part_copy(c, j).wait_send()

        @pl.when(feeds)
        def _():
            for j in range(peers):
                end_copy(c, j).wait_send()


def write_out(pair, own, pair_out, self_out, sem):
    copies = [pltpu.make_async_copy(src, dst, sem.at[n])
              for n, (src, dst) in enumerate(((pair, pair_out), (own, self_out)))]
    for copy in copies:
        copy.start()
    for copy in copies:
        copy.wait()


def store(pair, own):
    return pl.pallas_call(
        write_out,
        out_shape=(jax.ShapeDtypeStruct(pair.shape, F32), jax.ShapeDtypeStruct(own.shape, F32)),
        in_specs=[pl.BlockSpec(memory_space=pltpu.VMEM)] * 2,
        out_specs=(pl.BlockSpec(memory_space=pltpu.HBM),) * 2,
        scratch_shapes=[pltpu.SemaphoreType.DMA((2,))],
        compiler_params=pltpu.CompilerParams(vmem_limit_bytes=4 * 2**20),
    )(pair, own)


def per_device(slab, occ_density, virt_density, block_mask, matching):
    owners = lax.axis_size("aux")
    orbs = lax.axis_size("orb")
    reps = lax.axis_size("rep")
    chips = owners // 2
    aux_rows, batch, orb_cols = slab.shape
    rows_piece = aux_rows // max(2, 32 // chips)
    counts = (rows_piece,) * (aux_rows // rows_piece)
    pieces = len(counts)
    half = batch // reps
    rows_out = aux_rows // orbs
    self_cols = aux_rows // reps
    peers = orbs * reps
    factor = 1.0 / math.sqrt(batch * orb_cols * orbs)
    dma = pltpu.SemaphoreType.DMA
    vmem = pl.BlockSpec(memory_space=pltpu.VMEM)
    hbm = pl.BlockSpec(memory_space=pltpu.HBM)
    gathers = [pltpu.VMEM((owners, half, count, orb_cols), BF16) for count in counts]
    buffers = [
        ((aux_rows, batch, orb_cols), BF16),
        ((half, aux_rows, orb_cols), BF16),
        ((orb_cols, orb_cols), BF16),
        ((orb_cols, orb_cols), BF16),
        ((2, aux_rows, half * orb_cols), BF16),
        ((pieces, reps, orbs, rows_piece, rows_out), BF16),
        ((pieces, reps, orbs, rows_piece, rows_out), BF16),
        ((pieces, orbs, rows_piece, rows_out), F32),
        ((pieces, peers - 1, rows_piece, rows_out), BF16),
        ((pieces, peers, rows_piece, rows_out), BF16),
        ((reps, aux_rows, self_cols), BF16),
        ((aux_rows, self_cols), F32),
        ((peers - 1, rows_out, self_cols), BF16),
    ]
    held = sum(math.prod(shape) * jnp.dtype(kind).itemsize for shape, kind in buffers)
    held += owners * half * aux_rows * orb_cols * jnp.dtype(BF16).itemsize
    pair, own = pl.pallas_call(
        functools.partial(kernel, (chips, orbs, reps, counts), factor),
        out_shape=(
            jax.ShapeDtypeStruct((rows_out, aux_rows), F32),
            jax.ShapeDtypeStruct((rows_out, self_cols), F32),
        ),
        in_specs=[hbm] * 5,
        out_specs=(vmem, vmem),
        scratch_shapes=gathers + [
            pltpu.SMEM(matching.shape, matching.dtype), pltpu.SMEM(block_mask.shape, block_mask.dtype),
        ] + [pltpu.VMEM(shape, kind) for shape, kind in buffers] + [
            dma((2,)), dma((pieces,)), dma((2,)), dma((pieces,)), dma((pieces, chips)),
            dma((pieces, chips)), dma((pieces, chips)), dma((pieces, chips)), dma((pieces, chips)),
            dma((pieces, peers - 1)), dma((pieces, peers - 1)),
            dma((pieces, peers)), dma((pieces, peers)),
            dma((peers - 1,)), dma((peers - 1,)),
        ],
        compiler_params=pltpu.CompilerParams(
            collective_id=0, has_side_effects=True, vmem_limit_bytes=held + 8 * 2**20
        ),
    )(*(pltpu.with_memory_space_constraint(x, pltpu.HBM)
        for x in (matching, block_mask, slab, occ_density, virt_density)))
    return store(pair[None], own)


def solution(mesh):
    return jax.shard_map(
        per_device,
        mesh=mesh,
        in_specs=(P("aux", None, "orb"), P("orb", None), P("orb", None), P("aux", "orb"), P()),
        out_specs=(P("rep", ("aux", "orb"), None), P(("aux", "orb"), "rep")),
        check_vma=False,
    )
```

```python
import functools
import math

import jax
import jax.numpy as jnp
from jax import lax
from jax.experimental import pallas as pl
from jax.experimental.pallas import tpu as pltpu
from jax.sharding import PartitionSpec as P

BLOCK = 128
MESH = pl.DeviceIdType.MESH
CONTRACT = (((1,), (1,)), ((), ()))
F32, BF16 = jnp.float32, jnp.bfloat16


def kernel(sizes, factor, match_hbm, mask_hbm, slab, occ_hbm, virt_hbm, pair_out, self_out, *scratch):
    chips, orbs, reps, counts = sizes
    pieces = len(counts)
    firsts = [sum(counts[:c]) for c in range(pieces)]
    gath = scratch[:pieces]
    (match_ref, mask_ref, raw, masked, occ_dens, virt_dens, occ, parts, end_parts, whole, arrived, end_arrived,
     self_parts, self_whole, self_arrived, small_sem, raw_sem, dens_sem, local_sem, up_sem, down_sem,
     recv_sem, core_send, core_recv, part_send, part_recv, end_send, end_recv, self_send, self_recv) = scratch[pieces:]
    half, aux_rows, orb_cols = masked.shape
    rows_out = aux_rows // orbs
    self_cols = aux_rows // reps
    peers = orbs * reps

    a = lax.axis_index("aux")
    o = lax.axis_index("orb")
    r = lax.axis_index("rep")
    z = a // 2
    k = a % 2
    inner = jnp.logical_and(z >= 1, z <= chips - 2)
    at_end = jnp.logical_not(inner)
    feeds = jnp.logical_or(z == 1, z == chips - 2)
    end_aux = jnp.where(z == 1, k, 2 * (chips - 1) + k)
    feed_aux = jnp.where(z == 0, 2 + k, 2 * (chips - 2) + k)
    other = 2 * z + 1 - k
    up_ok = z + 1 <= chips - 2
    down_ok = z - 1 >= 1

    def peer(j):
        to_orb, to_rep = (o + j // reps) % orbs, (r + j % reps) % reps
        return to_orb, {"orb": to_orb, "rep": to_rep}

    def rows(c):
        return pl.ds(firsts[c], counts[c])

    def raw_copy(c):
        return pltpu.make_async_copy(slab.at[rows(c)], raw.at[rows(c)], raw_sem.at[c])

    mask_copy = pltpu.make_async_copy(mask_hbm, mask_ref, small_sem.at[0])
    match_copy = pltpu.make_async_copy(match_hbm, match_ref, small_sem.at[1])
    mask_copy.start()
    raw_copy(0).start()
    barrier = pltpu.get_barrier_semaphore()

    def greet(where):
        pl.semaphore_signal(barrier, inc=1, device_id=where, device_id_type=MESH)

    @pl.when(z > 0)
    def _():
        greet({"aux": a - 2})

    @pl.when(z < chips - 1)
    def _():
        greet({"aux": a + 2})

    greet({"aux": other})
    for j in range(1, peers):
        greet(peer(j)[1])

        @pl.when(feeds)
        def _():
            greet(dict(peer(j)[1], aux=end_aux))

        @pl.when(at_end)
        def _():
            greet(dict(peer(j)[1], aux=feed_aux))

    for c in range(1, pieces):
        raw_copy(c).start()
    match_copy.start()
    occ_copy = pltpu.make_async_copy(occ_hbm, occ_dens, dens_sem.at[0])
    virt_copy = pltpu.make_async_copy(virt_hbm, virt_dens, dens_sem.at[1])
    occ_copy.start()
    virt_copy.start()

    def remote(src, dst, send, recv, where):
        return pltpu.make_async_remote_copy(
            src_ref=src, dst_ref=dst, send_sem=send, recv_sem=recv, device_id=where, device_id_type=MESH
        )

    def piece(c):
        return masked.at[:, rows(c), :]

    def slot(c, owner):
        return gath[c].at[owner]

    def up(c, zz, src):
        return remote(src, slot(c, 2 * zz + k), up_sem.at[c, zz], recv_sem.at[c, zz], {"aux": a + 2})

    def down(c, zz, src):
        return remote(src, slot(c, 2 * zz + k), down_sem.at[c, zz], recv_sem.at[c, zz], {"aux": a - 2})

    def cross(c, zz, src):
        return remote(src, slot(c, 2 * zz + k), core_send.at[c, zz], core_recv.at[c, zz], {"aux": other})

    def local(c):
        return pltpu.make_async_copy(piece(c), slot(c, a), local_sem.at[c])

    def lower(c, send):
        for d in range(1, chips) if send else reversed(range(1, chips)):
            @pl.when(z - d >= 0)
            def _():
                zz = jnp.maximum(z - d, 0)
                up(c, zz, slot(c, 2 * zz + k)).wait_recv()
                if send:
                    up(c, zz, slot(c, 2 * zz + k)).start()
                cross(c, zz, slot(c, 2 * zz + k)).start()

    def upper(c, send):
        for d in range(1, chips) if send else reversed(range(1, chips)):
            @pl.when(z + d <= chips - 1)
            def _():
                zz = jnp.minimum(z + d, chips - 1)
                down(c, zz, slot(c, 2 * zz + k)).wait_recv()
                if send:
                    down(c, zz, slot(c, 2 * zz + k)).start()
                cross(c, zz, slot(c, 2 * zz + k)).start()

    def own(c):
        @pl.when(up_ok)
        def _():
            up(c, z, piece(c)).start()

        @pl.when(down_ok)
        def _():
            down(c, z, piece(c)).start()

    def relay(c):
        @pl.when(jnp.logical_and(inner, up_ok))
        def _():
            lower(c, True)

        @pl.when(jnp.logical_and(inner, down_ok))
        def _():
            upper(c, True)

        @pl.when(feeds)
        def _():
            occ[1, rows(c), :] = flat_dot(gath[c][end_aux], occ_dens)

    def complete(c):
        @pl.when(inner)
        def _():
            @pl.when(jnp.logical_not(up_ok))
            def _():
                lower(c, False)

            @pl.when(jnp.logical_not(down_ok))
            def _():
                upper(c, False)

    def part_copy(c, j):
        to_orb, where = peer(j)
        return remote(parts.at[c, j % reps, to_orb, pl.ds(0, counts[c])], arrived.at[c, j - 1, pl.ds(0, counts[c])],
                      part_send.at[c, j - 1], part_recv.at[c, j - 1], where)

    def end_copy(c, j):
        to_orb, where = peer(j)
        return remote(end_parts.at[c, j % reps, to_orb, pl.ds(0, counts[c])],
                      end_arrived.at[c, j, pl.ds(0, counts[c])],
                      end_send.at[c, j], end_recv.at[c, j], dict(where, aux=end_aux))

    def self_copy(j):
        to_orb, where = peer(j)
        return remote(self_parts.at[j % reps, pl.ds(to_orb * rows_out, rows_out), :], self_arrived.at[j - 1],
                      self_send.at[j - 1], self_recv.at[j - 1], where)

    def prepare(c):
        raw_copy(c).wait()
        chunk = min(counts[c], BLOCK // 2)
        for n in range(counts[c] // chunk):
            first = firsts[c] + n * chunk
            span = pl.ds(first, chunk)
            turned = pltpu.einshape("ald->lad", raw[span])
            block = first // BLOCK
            weight = jnp.concatenate(
                [jnp.full((chunk, BLOCK), mask_ref[block, b].astype(F32)) for b in range(orb_cols // BLOCK)], 1
            ).astype(BF16)
            for i in range(half):
                mine = turned[i]
                for q in range(1, reps):
                    mine = jnp.where(r == q, turned[q * half + i], mine)
                masked[i, span, :] = mine * weight

    def flat_dot(block, dens):
        count = block.shape[1]
        made = jnp.dot(block.reshape(half * count, orb_cols), dens[...], preferred_element_type=F32).astype(BF16)
        return jnp.concatenate([made[i * count:(i + 1) * count] for i in range(half)], 1)

    def self_tile(block):
        moved = flat_dot(block, virt_dens)
        return lax.dot_general(occ[0], moved, CONTRACT, preferred_element_type=F32) * factor

    def turned_tiles(c, which, owner):
        blocks = jnp.concatenate([gath[c][match_ref[(r + s) % reps, owner]] for s in range(reps)], 1)
        moved = flat_dot(blocks, virt_dens)
        total = lax.dot_general(moved, occ[which], CONTRACT, preferred_element_type=F32) * factor
        count = counts[c]
        return [[total[s * count:(s + 1) * count, q * rows_out:(q + 1) * rows_out]
                 for q in range(orbs)] for s in range(reps)]

    def gathered(c):
        @pl.when(inner)
        def _():
            for zz in range(chips):
                cross(c, zz, slot(c, 2 * zz + 1 - k)).wait_recv()
            local(c).wait()

    def end_tiles(c):
        @pl.when(feeds)
        def _():
            tiles = turned_tiles(c, 1, end_aux)
            for s in reversed(range(reps)):
                for q in range(orbs):
                    end_parts[c, s, q, :counts[c]] = tiles[s][q].astype(BF16)
            for j in reversed(range(peers)):
                end_copy(c, j).start()

    def own_tiles(c):
        @pl.when(inner)
        def _():
            tiles = turned_tiles(c, 0, a)
            for s in reversed(range(reps)):
                for q in range(orbs):
                    parts[c, s, q, :counts[c]] = tiles[s][q].astype(BF16)
                    if s == 0:
                        whole[c, q, :counts[c]] = tiles[s][q]
            for j in reversed(range(1, peers)):
                part_copy(c, j).start()

    def self_tiles():
        for s in reversed(range(reps)):
            side = (r + s) % reps
            total = self_tile(masked[:, pl.ds(side * self_cols, self_cols), :])
            self_parts[s] = total.astype(BF16)
            if s == 0:
                self_whole[...] = total
            for j in range(1, peers):
                if j % reps == s:
                    self_copy(j).start()

    def columns(c):
        return slice(firsts[c], firsts[c] + counts[c])

    def finish(c):
        @pl.when(inner)
        def _():
            total = whole[c, o, :counts[c]]
            for j in range(1, peers):
                part_copy(c, j).wait_recv()
                total = total + arrived[c, j - 1, :counts[c]].astype(F32)
            pair_out[:, columns(c)] = total.T

    def finish_end(c):
        @pl.when(at_end)
        def _():
            total = None
            for j in range(peers):
                end_copy(c, j).wait_recv()
                term = end_arrived[c, j, :counts[c]].astype(F32)
                total = term if total is None else total + term
            pair_out[:, columns(c)] = total.T

    def finish_self():
        total = self_whole[pl.ds(o * rows_out, rows_out), :]
        for j in range(1, peers):
            self_copy(j).wait_recv()
            total = total + self_arrived[j - 1].astype(F32)
        self_out[...] = total

    mask_copy.wait()
    for c in range(pieces):
        prepare(c)
        if c == 0:
            pl.semaphore_wait(
                barrier,
                peers + jnp.where(inner, 2, 1) + jnp.where(jnp.logical_or(feeds, at_end), peers - 1, 0),
            )
        if c < 4:
            own(c)

        @pl.when(inner)
        def _():
            cross(c, z, piece(c)).start()
            local(c).start()

    match_copy.wait()
    occ_copy.wait()
    virt_copy.wait()
    for c in range(pieces):
        occ[0, rows(c), :] = flat_dot(masked[:, rows(c), :], occ_dens)
    ahead = min(4, pieces)
    for c in range(ahead):
        relay(c)
        if c == 0:
            self_tiles()
    ended = 0
    lag = 3
    for c in range(pieces):
        if c + 4 < pieces:
            own(c + 4)
        if c + ahead < pieces:
            relay(c + ahead)
        filled = c + ahead >= pieces - 1
        while filled and ended < c:
            end_tiles(ended)
            ended += 1
        complete(c)
        gathered(c)
        if filled:
            end_tiles(c)
            ended += 1
        own_tiles(c)
        if c == 0:
            finish_self()
        if c >= lag:
            finish(c - lag)
    for c in range(max(0, pieces - lag), pieces):
        finish(c)
    for c in range(pieces):
        finish_end(c)

    for c in range(pieces):
        for d in range(chips):
            @pl.when(jnp.logical_and(up_ok, z - d >= 0))
            def _():
                up(c, jnp.maximum(z - d, 0), piece(c)).wait_send()

            @pl.when(jnp.logical_and(down_ok, z + d <= chips - 1))
            def _():
                down(c, jnp.minimum(z + d, chips - 1), piece(c)).wait_send()

        @pl.when(inner)
        def _():
            for zz in range(chips):
                cross(c, zz, piece(c)).wait_send()
    for j in range(1, peers):
        self_copy(j).wait_send()
    for c in range(pieces):
        @pl.when(inner)
        def _():
            for j in range(1, peers):
                part_copy(c, j).wait_send()

        @pl.when(feeds)
        def _():
            for j in range(peers):
                end_copy(c, j).wait_send()


def write_out(pair, own, pair_out, self_out, sem):
    copies = [pltpu.make_async_copy(src, dst, sem.at[n])
              for n, (src, dst) in enumerate(((pair, pair_out), (own, self_out)))]
    for copy in copies:
        copy.start()
    for copy in copies:
        copy.wait()


def store(pair, own):
    return pl.pallas_call(
        write_out,
        out_shape=(jax.ShapeDtypeStruct(pair.shape, F32), jax.ShapeDtypeStruct(own.shape, F32)),
        in_specs=[pl.BlockSpec(memory_space=pltpu.VMEM)] * 2,
        out_specs=(pl.BlockSpec(memory_space=pltpu.HBM),) * 2,
        scratch_shapes=[pltpu.SemaphoreType.DMA((2,))],
        compiler_params=pltpu.CompilerParams(vmem_limit_bytes=4 * 2**20),
    )(pair, own)


def per_device(slab, occ_density, virt_density, block_mask, matching):
    owners = lax.axis_size("aux")
    orbs = lax.axis_size("orb")
    reps = lax.axis_size("rep")
    chips = owners // 2
    aux_rows, batch, orb_cols = slab.shape
    rows_piece = aux_rows // max(2, 32 // chips)
    counts = (rows_piece,) * (aux_rows // rows_piece)
    pieces = len(counts)
    half = batch // reps
    rows_out = aux_rows // orbs
    self_cols = aux_rows // reps
    peers = orbs * reps
    factor = 1.0 / math.sqrt(batch * orb_cols * orbs)
    dma = pltpu.SemaphoreType.DMA
    vmem = pl.BlockSpec(memory_space=pltpu.VMEM)
    hbm = pl.BlockSpec(memory_space=pltpu.HBM)
    gathers = [pltpu.VMEM((owners, half, count, orb_cols), BF16) for count in counts]
    buffers = [
        ((aux_rows, batch, orb_cols), BF16),
        ((half, aux_rows, orb_cols), BF16),
        ((orb_cols, orb_cols), BF16),
        ((orb_cols, orb_cols), BF16),
        ((2, aux_rows, half * orb_cols), BF16),
        ((pieces, reps, orbs, rows_piece, rows_out), BF16),
        ((pieces, reps, orbs, rows_piece, rows_out), BF16),
        ((pieces, orbs, rows_piece, rows_out), F32),
        ((pieces, peers - 1, rows_piece, rows_out), BF16),
        ((pieces, peers, rows_piece, rows_out), BF16),
        ((reps, aux_rows, self_cols), BF16),
        ((aux_rows, self_cols), F32),
        ((peers - 1, rows_out, self_cols), BF16),
    ]
    held = sum(math.prod(shape) * jnp.dtype(kind).itemsize for shape, kind in buffers)
    held += owners * half * aux_rows * orb_cols * jnp.dtype(BF16).itemsize
    pair, own = pl.pallas_call(
        functools.partial(kernel, (chips, orbs, reps, counts), factor),
        out_shape=(
            jax.ShapeDtypeStruct((rows_out, aux_rows), F32),
            jax.ShapeDtypeStruct((rows_out, self_cols), F32),
        ),
        in_specs=[hbm] * 5,
        out_specs=(vmem, vmem),
        scratch_shapes=gathers + [
            pltpu.SMEM(matching.shape, matching.dtype), pltpu.SMEM(block_mask.shape, block_mask.dtype),
        ] + [pltpu.VMEM(shape, kind) for shape, kind in buffers] + [
            dma((2,)), dma((pieces,)), dma((2,)), dma((pieces,)), dma((pieces, chips)),
            dma((pieces, chips)), dma((pieces, chips)), dma((pieces, chips)), dma((pieces, chips)),
            dma((pieces, peers - 1)), dma((pieces, peers - 1)),
            dma((pieces, peers)), dma((pieces, peers)),
            dma((peers - 1,)), dma((peers - 1,)),
        ],
        compiler_params=pltpu.CompilerParams(
            collective_id=0, has_side_effects=True, vmem_limit_bytes=held + 8 * 2**20
        ),
    )(*(pltpu.with_memory_space_constraint(x, pltpu.HBM)
        for x in (matching, block_mask, slab, occ_density, virt_density)))
    return store(pair[None], own)


def solution(mesh):
    return jax.shard_map(
        per_device,
        mesh=mesh,
        in_specs=(P("aux", None, "orb"), P("orb", None), P("orb", None), P("aux", "orb"), P()),
        out_specs=(P("rep", ("aux", "orb"), None), P(("aux", "orb"), "rep")),
        check_vma=False,
    )
```
